32 devices in a mesh: frame: 8 (over y, x, core), tensor: 4 (over z).
Axes of the slice: x: 2, y: 2, z: 4, core: 2. Of those that a mesh axis runs over, the one named last changes fastest.
Arguments:
- hidden: bfloat16 [8192, 3072], P(('frame', 'tensor')), may hold values from -6 to 6
- qkv_weight: bfloat16 [3072, 3, 3072], P(None, None, 'tensor'), may hold values from -0.109375 to 0.109375
- norm_gain: float32 [2, 128], replicated, may hold values from 0.5 to 10, as said below
- out_grad: bfloat16 [8192, 3072], P('frame', 'tensor'), may hold values from -0.15625 to 0.15625
Outputs:
- attended: bfloat16 [8192, 3072], P('frame', 'tensor')
- weight_grad: float32 [3072, 3, 3072], P('frame', None, 'tensor')
The draws below stay inside these ranges and needn't reach their ends.
Inputs may be any that keep to these rules, and one draw needn't show every extreme that they name: `norm_gain`: every gain is positive.
All inputs are finite; a program needn't handle non-finite values.
Results may differ from the reference program's by a relative error of at most 0.028.
The reference program's roundings to bfloat16 on the way (of `weights`, `score_grads` and `qkv_grad`) count: a program that leaves them out, or rounds other values in their place, can miss the bound.
Values may be sent and summed in bfloat16 or wider, within the bound.
A program may use at most 192 MiB of HBM per device.

```python
import math
import jax
import jax.numpy as jnp
from jax import lax

HEAD_DIM = 128
D = 3072
GROUP = 1024
TOKENS = 8192
N_FRAME = 8


def draw_norm_gain(key, part):
    return jnp.exp(jax.random.uniform(key, (2, HEAD_DIM), jnp.float32, math.log(0.6), math.log(1.8)))


def strengthened(values, stream_key, source, target, parts, factor):
    def block_of(dim):
        return (jnp.arange(values.shape[dim]) // (values.shape[dim] // parts)).reshape((-1,) + (1,) * (values.ndim - 1 - dim))

    first = jax.random.permutation(stream_key, parts)[block_of(target)]
    far = (block_of(target) + parts // 2) % parts
    return jnp.where((block_of(source) == first) | (block_of(source) == far), factor * values, values)


def shard_levels(rng, extent, pieces, least, high):
    def one(position, parts):
        draws = jax.random.uniform(jax.random.fold_in(jax.random.fold_in(rng, 6), position), (parts,), jnp.float32, least / len(pieces), high / len(pieces))
        return jnp.repeat(jnp.exp(draws), extent[position] // parts).reshape((-1,) + (1,) * (len(extent) - position - 1))

    loudness = one(*pieces[0])
    for cut in pieces[1:]:
        loudness = loudness * one(*cut)
    return loudness


def gaussian(stream_key, extent, spread, most, cuts=(), kind=jnp.bfloat16):
    result = spread * jax.random.normal(stream_key, extent, jnp.float32)
    if cuts:
        result = result * shard_levels(stream_key, extent, cuts, -0.22, 0.18)
    return jnp.clip(result, -most, most).astype(kind)


def noise_with(key, shape, scale, limit, pieces, heavy, held_as=jnp.bfloat16):
    drawn = scale * jax.random.normal(key, shape, jnp.float32)
    if pieces:
        drawn = drawn * shard_levels(key, shape, pieces, -0.22, 0.18)
    return jnp.clip(strengthened(drawn, jax.random.fold_in(key, 3), *heavy), -limit, limit).astype(held_as)


def setup_inputs(seed: int = 0) -> dict:
    seeds = jax.random.split(jax.random.key(seed), 5)
    hidden = noise_with(seeds[0], (TOKENS, D), 1.0, 6.0, ((0, 32),), (0, 1, 32, 2.75))
    qkv_weight = gaussian(seeds[1], (D, 3, D), D ** -0.5, 0.109375, ((2, 4),))
    norm_gain = draw_norm_gain(jax.random.fold_in(seeds[4], 71), 0)
    out_grad = gaussian(seeds[3], (TOKENS, D), (TOKENS ** -0.5), 0.15625, ((0, 8), (1, 4)))
    return dict(hidden=hidden, qkv_weight=qkv_weight, norm_gain=norm_gain, out_grad=out_grad)


EPSILON = 1e-06

def norm_heads(projected, gain):
    inverse_rms = lax.rsqrt(lax.optimization_barrier(jnp.mean(projected * projected, axis=-1, keepdims=True)) + EPSILON)
    return (projected * inverse_rms * gain, inverse_rms)

def norm_back(projected, inverse_rms, gain, grad):
    weighted = grad * gain
    inner = lax.optimization_barrier(jnp.mean(projected * weighted, axis=-1, keepdims=True))
    return inverse_rms * weighted - projected * (inverse_rms * inverse_rms * inverse_rms) * inner

def product(form, left, right):
    return jnp.einsum(form, left.astype(jnp.float32), right.astype(jnp.float32))

def window_attention(query, window, out_grad, valid):
    total_rows = query.shape[0]
    block = min(512, total_rows)
    keys = window[:, 0]
    values = window[:, 1]
    factor = query.shape[-1] ** (-0.5)
    output_list = []
    query_grads = []
    keyval_grad = jnp.zeros(window.shape, jnp.float32)
    for first_row in range(0, total_rows, block):
        query_block = query[first_row:first_row + block]
        grad_block = out_grad[first_row:first_row + block]
        scores = product('qhd,khd->hqk', query_block, keys) * factor
        scores = jnp.where(valid[None, None, :], scores, -1e+30)
        peak = lax.optimization_barrier(jnp.max(scores, axis=-1, keepdims=True))
        raised = jnp.exp(scores - peak)
        weights = (raised / lax.optimization_barrier(jnp.sum(raised, axis=-1, keepdims=True))).astype(jnp.bfloat16)
        attended = product('hqk,khd->qhd', weights, values).astype(jnp.bfloat16)
        row_dots = lax.optimization_barrier(jnp.sum(grad_block.astype(jnp.float32) * attended.astype(jnp.float32), axis=-1))
        prob_grads = product('qhd,khd->hqk', grad_block, values)
        score_grads = (weights.astype(jnp.float32) * (prob_grads - row_dots.T[:, :, None])).astype(jnp.bfloat16)
        query_grad = product('hqk,khd->qhd', score_grads, keys) * factor
        key_grad = product('hqk,qhd->khd', score_grads, query_block) * factor
        value_grad = product('hqk,qhd->khd', weights, grad_block)
        keyval_grad = keyval_grad + jnp.stack([key_grad, value_grad], axis=1)
        output_list.append(attended)
        query_grads.append(query_grad)
    return (jnp.concatenate(output_list, 0), jnp.concatenate(query_grads, 0), keyval_grad)

def reference(hidden, qkv_weight, norm_gain, out_grad):
    tokens, width = hidden.shape
    heads = width // HEAD_DIM
    projected = jnp.dot(hidden, qkv_weight.reshape(width, 3 * width), preferred_element_type=jnp.float32)
    projected = projected.reshape(tokens, 3, heads, HEAD_DIM)
    query_normed, query_rms = norm_heads(projected[:, 0], norm_gain[0])
    key_normed, key_rms = norm_heads(projected[:, 1], norm_gain[1])
    query = query_normed.astype(jnp.bfloat16)
    keyval = jnp.stack([key_normed.astype(jnp.bfloat16), projected[:, 2].astype(jnp.bfloat16)], 1)
    half = GROUP // 2
    padded = jnp.pad(keyval, ((half, half), (0, 0), (0, 0), (0, 0)))
    grads_heads = out_grad.reshape(tokens, heads, HEAD_DIM)

    def one_group(group_index):
        start = (group_index * GROUP).astype(jnp.int32)
        window = lax.dynamic_slice_in_dim(padded, start, 2 * GROUP, 0)
        query_rows = lax.dynamic_slice_in_dim(query, start, GROUP, 0)
        grad_rows = lax.dynamic_slice_in_dim(grads_heads, start, GROUP, 0)
        place = start + jnp.arange(2 * GROUP, dtype=jnp.int32)
        valid = (place >= half) & (place < tokens + half)
        return window_attention(query_rows, window, grad_rows, valid)
    outputs, query_grads, keyval_grads = lax.map(one_group, jnp.arange(N_FRAME, dtype=jnp.int32))
    lower = keyval_grads[:, :half]
    own = keyval_grads[:, half:half + GROUP]
    upper = keyval_grads[:, half + GROUP:]
    zero_rows = jnp.zeros_like(lower[:1])
    from_prev = jnp.concatenate([zero_rows, upper[:-1]], 0)
    from_next = jnp.concatenate([lower[1:], zero_rows], 0)
    keyval_grad = (own + jnp.concatenate([from_prev, from_next], 1)).reshape(tokens, 2, heads, HEAD_DIM)
    query_grad = query_grads.reshape(tokens, heads, HEAD_DIM)
    query_raw_grad = norm_back(projected[:, 0], query_rms, norm_gain[0], query_grad)
    key_raw_grad = norm_back(projected[:, 1], key_rms, norm_gain[1], keyval_grad[:, 0])
    qkv_grad = jnp.stack([query_raw_grad, key_raw_grad, keyval_grad[:, 1]], 1).astype(jnp.bfloat16)
    qkv_grad = qkv_grad.reshape(tokens, 3 * width)
    weight_grad = jnp.dot(hidden.T, qkv_grad, preferred_element_type=jnp.float32).reshape(width, 3, width)
    return (outputs.reshape(tokens, width), weight_grad)
```

```python
import functools
import math

import jax
import jax.numpy as jnp
from jax import lax
from jax.experimental import pallas as pl
from jax.experimental.pallas import tpu as pltpu
from jax.sharding import PartitionSpec as P

HEAD_DIM = 128
EPSILON = 1e-06
MASKED = -1e30
NT = (((1,), (1,)), ((), ()))


def ppermute_by(value, axis, steps):
    count = lax.axis_size(axis)
    initial, last = (max(0, -steps), min(count, count - steps))
    return lax.ppermute(value, axis, [(source, source + steps) for source in range(initial, last)])


def inverse_rms_of(raw):
    return lax.rsqrt(jnp.mean(raw * raw, axis=-1, keepdims=True) + EPSILON)


def norm_back(raw, inverse_rms, gain, grad):
    weighted = grad * gain
    inner = jnp.mean(raw * weighted, axis=-1, keepdims=True)
    return inverse_rms * weighted - raw * (inverse_rms * inverse_rms * inverse_rms) * inner


def dot32(left, right):
    return jnp.dot(left, right, preferred_element_type=jnp.float32)


def dot_nt(left, right):
    return lax.dot_general(left, right, NT, preferred_element_type=jnp.float32)


MESH = pl.DeviceIdType.MESH


def flipped(index, bit):
    return index + bit - 2 * bit * (index // bit % 2)


def halving_orders(count):
    bits = [1 << i for i in range(count.bit_length() - 1)]
    return [bits, bits[:1] + bits[:0:-1]]


def attend_kernel(
    count, gain_ref, raw_ref, kraw_ref, grad_ref, kp_ref, ko_ref, kn_ref, vp_ref, vo_ref, vn_ref, turned_ref,
    att_ref, sum_ref,
    kt, vt, score, prob_grad, weight, dk_acc, dv_acc, grads, edge_out, edge_in, terms, landed,
    edge_send, edge_recv, send_sems, recv_sems,
):
    half = kp_ref.shape[0]
    block = score.shape[1]
    blocks = ko_ref.shape[0] // block
    heads = ko_ref.shape[1] // HEAD_DIM
    factor = HEAD_DIM ** (-0.5)
    scale = factor * math.log2(math.e)
    orders = halving_orders(count)
    streams, levels = len(orders), len(orders[0])
    piece = terms.shape[3]
    me = lax.axis_index("frame")
    has_prev, has_next = me > 0, me < count - 1
    bias_prev = jnp.where(has_prev, 0.0, MASKED).astype(jnp.float32)
    bias_next = jnp.where(has_next, 0.0, MASKED).astype(jnp.float32)

    barrier = pltpu.get_barrier_semaphore()
    for bit in orders[0]:
        pl.semaphore_signal(barrier, inc=1, device_id={"frame": flipped(me, bit)}, device_id_type=MESH)
    for near, there in ((has_prev, me - 1), (has_next, me + 1)):
        @pl.when(near)
        def _(there=there):
            pl.semaphore_signal(barrier, inc=1, device_id={"frame": there}, device_id_type=MESH)

    for side, near in ((0, has_next), (1, has_prev)):
        @pl.when(jnp.logical_not(near))
        def _(side=side):
            edge_in[:, side] = jnp.zeros(edge_in.shape[:1] + edge_in.shape[2:], edge_in.dtype)

    pl.semaphore_wait(barrier, levels + has_prev.astype(jnp.int32) + has_next.astype(jnp.int32))

    def columns_of(head):
        return pl.ds(pl.multiple_of(head * HEAD_DIM, HEAD_DIM), HEAD_DIM)

    def edge_copy(side, slot):
        return pltpu.make_async_remote_copy(
            src_ref=edge_out.at[slot, side],
            dst_ref=edge_in.at[slot, side],
            send_sem=edge_send.at[slot, side],
            recv_sem=edge_recv.at[slot, side],
            device_id={"frame": me - 1 + 2 * side},
            device_id_type=MESH,
        )

    def attend_block(step):
        head, part = step // blocks, step % blocks
        slot = head % 2
        columns = columns_of(head)
        rows = pl.ds(pl.multiple_of(part * block, block), block)
        chunks = [
            (kp_ref, vp_ref, slice(0, half), bias_prev),
            (ko_ref, vo_ref, slice(0, half), None),
            (ko_ref, vo_ref, slice(half, 2 * half), None),
            (kn_ref, vn_ref, slice(0, half), bias_next),
        ]

        @pl.when(part == 0)
        def _():
            for i, (k_ref, v_ref, chunk, _) in enumerate(chunks):
                kt[:, i * half : (i + 1) * half] = k_ref[chunk, columns].T
                vt[:, i * half : (i + 1) * half] = v_ref[chunk, columns].T
            dk_acc[slot] = jnp.zeros(dk_acc.shape[1:], jnp.float32)
            dv_acc[slot] = jnp.zeros(dv_acc.shape[1:], jnp.float32)

        raw = raw_ref[rows, columns]
        gain = gain_ref[0:1]
        inverse_rms = inverse_rms_of(raw)
        query = (raw * inverse_rms * gain).astype(jnp.bfloat16)
        grad = grad_ref[rows, columns]
        peak = None
        for i, (k_ref, v_ref, chunk, bias) in enumerate(chunks):
            place = slice(i * half, (i + 1) * half)
            s = dot_nt(k_ref[chunk, columns], query)
            if bias is not None:
                s = s + bias
            score[place] = s
            top = jnp.max(s, axis=0, keepdims=True)
            peak = top if peak is None else jnp.maximum(peak, top)
        norm = None
        for i, (k_ref, v_ref, chunk, _) in enumerate(chunks):
            place = slice(i * half, (i + 1) * half)
            raised = jnp.exp2((score[place] - peak) * scale)
            score[place] = raised
            total = jnp.sum(raised, axis=0, keepdims=True)
            norm = total if norm is None else norm + total
            prob_grad[place] = dot_nt(v_ref[chunk, columns], grad)
        inverse = 1.0 / norm
        attended = None
        for i in range(4):
            place = slice(i * half, (i + 1) * half)
            w = (score[place] * inverse).astype(jnp.bfloat16)
            weight[place] = w
            term = dot32(vt[:, place], w)
            attended = term if attended is None else attended + term
            dv_acc[slot, place] += dot32(w, grad)
        attended = attended.T.astype(jnp.bfloat16)
        att_ref[rows, columns] = attended
        dots = jnp.sum((grad.astype(jnp.float32) * attended.astype(jnp.float32)).T, axis=0, keepdims=True)
        query_grad = None
        for i in range(4):
            place = slice(i * half, (i + 1) * half)
            ds = (weight[place].astype(jnp.float32) * (prob_grad[place] - dots)).astype(jnp.bfloat16)
            term = dot32(kt[:, place], ds)
            query_grad = term if query_grad is None else query_grad + term
            dk_acc[slot, place] += dot32(ds, query)
        query_grad = query_grad.T * factor
        grads[slot, rows, 0:HEAD_DIM] = norm_back(raw, inverse_rms, gain, query_grad).astype(jnp.bfloat16)

        @pl.when(part == blocks - 1)
        def _():
            for side, near in ((0, has_prev), (1, has_next)):
                place = slice(side * 3 * half, (side * 3 + 1) * half)

                @pl.when(near)
                def _(side=side, place=place):
                    edge_out[slot, side, 0] = (dk_acc[slot, place] * factor).astype(jnp.bfloat16)
                    edge_out[slot, side, 1] = dv_acc[slot, place].astype(jnp.bfloat16)
                    edge_copy(side, slot).start()

    def halving_copy(head, level, stream):
        near, far = terms.shape[2] >> (level + 1), terms.shape[2] >> level
        first = terms.shape[2] - far
        return pltpu.make_async_remote_copy(
            src_ref=terms.at[head % terms.shape[0], stream, pl.ds(near, far - near)],
            dst_ref=landed.at[head % landed.shape[0], stream, pl.ds(first, near)],
            send_sem=send_sems.at[head % terms.shape[0], stream, level],
            recv_sem=recv_sems.at[head % landed.shape[0], stream, level],
            device_id={"frame": flipped(me, orders[stream][level])},
            device_id_type=MESH,
        )

    def weight_terms(head):
        slot = head % 2
        columns = columns_of(head)
        for side, near in ((0, has_next), (1, has_prev)):
            @pl.when(near)
            def _(side=side):
                edge_copy(side, slot).wait_recv()
        gain = gain_ref[1:2]
        for part in range(2):
            rows = slice(part * half, (part + 1) * half)
            inner = slice((part + 1) * half, (part + 2) * half)
            raw = kraw_ref[rows, columns]
            grad = dk_acc[slot, inner] * factor + edge_in[slot, 1 - part, 0].astype(jnp.float32)
            back = norm_back(raw, inverse_rms_of(raw), gain, grad)
            grads[slot, rows, HEAD_DIM : 2 * HEAD_DIM] = back.astype(jnp.bfloat16)
            grad = dv_acc[slot, inner] + edge_in[slot, 1 - part, 1].astype(jnp.float32)
            grads[slot, rows, 2 * HEAD_DIM : 3 * HEAD_DIM] = grad.astype(jnp.bfloat16)
        for side, near in ((0, has_prev), (1, has_next)):
            @pl.when(near)
            def _(side=side):
                edge_copy(side, slot).wait_send()

        def one_pair(pair, carry):
            rows = pl.ds(pl.multiple_of(pair * 4 * piece, 4 * piece), 4 * piece)
            term = dot32(turned_ref[rows], grads[slot]).astype(jnp.bfloat16)
            for i in range(2):
                frame = 2 * pair + i
                for stream in range(streams):
                    place = 0
                    for bit in orders[stream]:
                        place = 2 * place + (frame // bit + me // bit) % 2
                    first = (2 * i + stream) * piece
                    terms[head % terms.shape[0], stream, place] = term[first : first + piece]
            return carry

        lax.fori_loop(0, count // 2, one_pair, 0)
        for stream in range(streams):
            halving_copy(head, 0, stream).start()

    def halve(head, level):
        slot, land = head % terms.shape[0], head % landed.shape[0]
        near, far = terms.shape[2] >> (level + 1), terms.shape[2] >> level
        for stream in range(streams):
            halving_copy(head, level - 1, stream).wait_recv()
            places = pl.ds(near, far - near)
            total = terms[slot, stream, places].astype(jnp.float32)
            for earlier in range(level):
                first = terms.shape[2] - (terms.shape[2] >> earlier)
                total += landed[land, stream, pl.ds(first + near, far - near)].astype(jnp.float32)
            terms[slot, stream, places] = total.astype(terms.dtype)
            halving_copy(head, level, stream).start()

    def finish(head):
        slot, land = head % terms.shape[0], head % landed.shape[0]
        columns = columns_of(head)
        for stream in range(streams):
            halving_copy(head, levels - 1, stream).wait_recv()
            total = terms[slot, stream, 0].astype(jnp.float32)
            for earlier in range(levels):
                first = terms.shape[2] - (terms.shape[2] >> earlier)
                total += landed[land, stream, first].astype(jnp.float32)
            for i in range(3):
                sum_ref[i, stream * piece : (stream + 1) * piece, columns] = total[:, i * HEAD_DIM : (i + 1) * HEAD_DIM]
        for stream in range(streams):
            for level in range(levels):
                halving_copy(head, level, stream).wait_send()

    def one_step(step, carry):
        @pl.when(step < heads * blocks)
        def _():
            attend_block(step)

        for level in range(levels, -1, -1):
            since = step - blocks - level
            head = since // blocks

            @pl.when((since >= 0) & (since % blocks == 0) & (head < heads))
            def _(level=level, head=head):
                if level == levels:
                    finish(head)
                elif level:
                    halve(head, level)
                else:
                    weight_terms(head)

        return carry

    lax.fori_loop(0, heads * blocks + levels + 1, one_step, 0)


def attend(gain, raw, kraw, grad, kp, ko, kn, vp, vo, vn, turned):
    count = lax.axis_size("frame")
    rows, local = raw.shape
    depth = turned.shape[0]
    heads, half = local // HEAD_DIM, rows // 2
    block = min(512, rows)
    window = 2 * rows
    levels = count.bit_length() - 1
    slots = -(-levels // (rows // block))
    piece = depth // count // 2
    vmem = pl.BlockSpec(memory_space=pltpu.VMEM)
    flops = 12 * rows * window * local + 6 * rows * depth * local
    return pl.pallas_call(
        functools.partial(attend_kernel, count),
        in_specs=[vmem] * 11,
        out_specs=(vmem, vmem),
        out_shape=(
            jax.ShapeDtypeStruct((rows, local), jnp.bfloat16),
            jax.ShapeDtypeStruct((3, depth // count, local), jnp.float32),
        ),
        scratch_shapes=[
            pltpu.VMEM((HEAD_DIM, window), jnp.bfloat16),
            pltpu.VMEM((HEAD_DIM, window), jnp.bfloat16),
            pltpu.VMEM((window, block), jnp.float32),
            pltpu.VMEM((window, block), jnp.float32),
            pltpu.VMEM((window, block), jnp.bfloat16),
            pltpu.VMEM((2, window, HEAD_DIM), jnp.float32),
            pltpu.VMEM((2, window, HEAD_DIM), jnp.float32),
            pltpu.VMEM((2, rows, 3 * HEAD_DIM), jnp.bfloat16),
            pltpu.VMEM((2, 2, 2, half, HEAD_DIM), jnp.bfloat16),
            pltpu.VMEM((2, 2, 2, half, HEAD_DIM), jnp.bfloat16),
            pltpu.VMEM((slots, 2, count, piece, 3 * HEAD_DIM), jnp.bfloat16),
            pltpu.VMEM((slots + 1, 2, count - 1, piece, 3 * HEAD_DIM), jnp.bfloat16),
            pltpu.SemaphoreType.DMA((2, 2)),
            pltpu.SemaphoreType.DMA((2, 2)),
            pltpu.SemaphoreType.DMA((slots, 2, levels)),
            pltpu.SemaphoreType.DMA((slots + 1, 2, levels)),
        ],
        compiler_params=pltpu.CompilerParams(
            collective_id=0, has_side_effects=True, vmem_limit_bytes=62 * 1024 * 1024
        ),
        cost_estimate=pl.CostEstimate(
            flops=flops, bytes_accessed=16 * rows * local, transcendentals=rows * window * heads
        ),
        name="attend",
    )(gain, raw, kraw, grad, kp, ko, kn, vp, vo, vn, turned)


def project_kernel(
    count, gain_ref, hidden_ref, weight_hbm, turned, query_raw, key_raw, keys, values,
    gathered, weight, weight_sems, send_sems, recv_sems,
):
    me = lax.axis_index("tensor")
    rows = hidden_ref.shape[0]
    has_left, has_right = me > 0, me < count - 1
    loads = [
        pltpu.make_async_copy(weight_hbm.at[i], weight.at[i], weight_sems.at[i]) for i in range(3)
    ]
    for load in loads:
        load.start()
    barrier = pltpu.get_barrier_semaphore()
    for there in (lax.rem(me + count - 1, count), lax.rem(me + 1, count)):
        pl.semaphore_signal(barrier, inc=1, device_id={"tensor": there}, device_id_type=MESH)
    pl.semaphore_wait(barrier, 2)

    def rows_of(shard):
        return pl.ds(pl.multiple_of(shard * rows, rows), rows)

    def copy_of(side, step, shard, source):
        return pltpu.make_async_remote_copy(
            src_ref=source,
            dst_ref=gathered.at[rows_of(shard)],
            send_sem=send_sems.at[side, step],
            recv_sem=recv_sems.at[side, step],
            device_id={"tensor": me + 1 - 2 * side},
            device_id_type=MESH,
        )

    for side, near in ((0, has_right), (1, has_left)):
        @pl.when(near)
        def _(side=side):
            copy_of(side, 0, me, hidden_ref).start()
    gathered[rows_of(me)] = hidden_ref[...]
    for load in loads:
        load.wait()

    def one_step(step, carry):
        @pl.when(step > 0)
        def _():
            for side, near in ((0, has_right), (1, has_left)):
                shard = me - step if side == 0 else me + step
                there = shard >= 0 if side == 0 else shard < count

                @pl.when(there)
                def _(side=side, shard=shard):
                    copy_of(side, step - 1, shard, gathered.at[rows_of(shard)]).wait_recv()

                @pl.when(there & near)
                def _(side=side, shard=shard):
                    copy_of(side, step, shard, gathered.at[rows_of(shard)]).start()

        def one_side(side, inner):
            shard = me - step + 2 * step * side

            @pl.when((shard >= 0) & (shard < count) & (step >= side))
            def _():
                place = rows_of(shard)
                tokens = gathered[place]
                raw = dot32(tokens, weight[1])
                key_raw[place] = raw
                for h in range(raw.shape[1] // HEAD_DIM):
                    columns = slice(h * HEAD_DIM, (h + 1) * HEAD_DIM)
                    head = raw[:, columns]
                    normed = head * inverse_rms_of(head) * gain_ref[1:2]
                    keys[place, columns] = normed.astype(keys.dtype)
                values[place] = dot32(tokens, weight[2]).astype(values.dtype)
                query_raw[place] = dot32(tokens, weight[0])
                turned[:, place] = tokens.T

            return inner

        return lax.fori_loop(0, 2, one_side, carry)

    lax.fori_loop(0, count, one_step, 0)
    for step in range(count - 1):
        for side, near in ((0, has_right), (1, has_left)):
            shard = me - step if side == 0 else me + step
            there = shard >= 0 if side == 0 else shard < count

            @pl.when(there & near)
            def _(side=side, shard=shard, step=step):
                source = hidden_ref if step == 0 else gathered.at[rows_of(shard)]
                copy_of(side, step, shard, source).wait_send()


def project(hidden, qkv_weight, gain):
    count = lax.axis_size("tensor")
    rows, depth = hidden.shape
    local = qkv_weight.shape[2]
    total = rows * count
    vmem = pl.BlockSpec(memory_space=pltpu.VMEM)
    wide = jax.ShapeDtypeStruct((total, local), jnp.float32)
    narrow = jax.ShapeDtypeStruct((total, local), jnp.bfloat16)
    return pl.pallas_call(
        functools.partial(project_kernel, count),
        in_specs=[vmem, vmem, pl.BlockSpec(memory_space=pl.ANY)],
        out_specs=(vmem,) * 5,
        out_shape=(jax.ShapeDtypeStruct((depth, total), hidden.dtype), wide, wide, narrow, narrow),
        scratch_shapes=[
            pltpu.VMEM((total, depth), hidden.dtype),
            pltpu.VMEM((3, depth, local), qkv_weight.dtype),
            pltpu.SemaphoreType.DMA((3,)),
            pltpu.SemaphoreType.DMA((2, count)),
            pltpu.SemaphoreType.DMA((2, count)),
        ],
        compiler_params=pltpu.CompilerParams(
            collective_id=1, has_side_effects=True, vmem_limit_bytes=50 * 1024 * 1024
        ),
        name="project",
    )(gain, hidden, jnp.transpose(qkv_weight, (1, 0, 2)))


def per_device(hidden, qkv_weight, norm_gain, out_grad):
    turned, query_raw, key_raw, keys, values = project(hidden, qkv_weight, norm_gain)
    rows = turned.shape[1]
    half = rows // 2
    kp, vp = (ppermute_by(a[rows - half :], "frame", 1) for a in (keys, values))
    kn, vn = (ppermute_by(a[:half], "frame", -1) for a in (keys, values))
    attended, sums = attend(
        norm_gain, query_raw, key_raw, out_grad, kp, keys, kn, vp, values, vn, turned
    )
    return (attended, jnp.transpose(sums, (1, 0, 2)))


def solution(mesh):
    placed = (P(("frame", "tensor"), None), P(None, None, "tensor"), P(), P("frame", "tensor"))
    return jax.shard_map(
        per_device,
        mesh=mesh,
        in_specs=placed,
        out_specs=(P("frame", "tensor"), P("frame", None, "tensor")),
        check_vma=False,
    )
```

```python
import functools
import math

import jax
import jax.numpy as jnp
from jax import lax
from jax.experimental import pallas as pl
from jax.experimental.pallas import tpu as pltpu
from jax.sharding import PartitionSpec as P

HEAD_DIM = 128
EPSILON = 1e-06
MASKED = -1e30
NT = (((1,), (1,)), ((), ()))


def inverse_rms_of(raw):
    return lax.rsqrt(jnp.mean(raw * raw, axis=-1, keepdims=True) + EPSILON)


def norm_back(raw, inverse_rms, gain, grad):
    weighted = grad * gain
    inner = jnp.mean(raw * weighted, axis=-1, keepdims=True)
    return inverse_rms * weighted - raw * (inverse_rms * inverse_rms * inverse_rms) * inner


def dot32(left, right):
    return jnp.dot(left, right, preferred_element_type=jnp.float32)


def dot_nt(left, right):
    return lax.dot_general(left, right, NT, preferred_element_type=jnp.float32)


MESH = pl.DeviceIdType.MESH


def flipped(index, bit):
    return index + bit - 2 * bit * (index // bit % 2)


def halving_orders(count):
    bits = [1 << i for i in range(count.bit_length() - 1)]
    return [bits, bits[:1] + bits[:0:-1]]


def aligned(first, size, unit):
    return pl.ds(pl.multiple_of(first, unit), size)


def block_kernel(
    count, shards, slots, lands, lag, per, gain_ref, hidden_hbm, weight_hbm, grad_ref,
    att_ref, sum_hbm,
    pool, gathered, turned, query_raw, key_raw, kv, kv_edge,
    kt, vt, score, prob_grad, weight, dk_acc, dv_acc, grads, edge_out, edge_in, totals,
    load_sems, own_sem, z_send, z_recv, kv_send, kv_recv, edge_send, edge_recv, send_sems, recv_sems,
    out_sems, ready,
):
    heads, _, tokens, _ = kv.shape
    half = tokens // 2
    rows, depth = gathered.shape[1:]
    block = score.shape[1]
    blocks = tokens // block
    chunk = min(128, rows)
    factor = HEAD_DIM ** (-0.5)
    scale = factor * math.log2(math.e)
    orders = halving_orders(count)
    streams, levels = len(orders), len(orders[0])
    piece = depth // count // streams
    group = 3 * HEAD_DIM
    edges = edge_in.shape[0]
    landed_base = slots * (streams // per) * count * piece
    me, mine_z = lax.axis_index("frame"), lax.axis_index("tensor")
    has_prev, has_next = me > 0, me < count - 1
    has_left, has_right = mine_z > 0, mine_z < shards - 1
    bias_prev = jnp.where(has_prev, 0.0, MASKED).astype(jnp.float32)
    bias_next = jnp.where(has_next, 0.0, MASKED).astype(jnp.float32)
    sides = ((0, has_prev), (1, has_next))
    ways = ((0, has_right), (1, has_left))

    loads = [
        pltpu.make_async_copy(weight_hbm.at[i], pool.at[pl.ds(i * depth, depth)], load_sems.at[i]) for i in range(3)
    ]
    own = pltpu.make_async_copy(hidden_hbm, gathered.at[mine_z], own_sem)
    own.start()
    for i in (1, 2, 0):
        loads[i].start()

    barrier = pltpu.get_barrier_semaphore()
    for bit in orders[0]:
        pl.semaphore_signal(barrier, inc=1, device_id={"frame": flipped(me, bit)}, device_id_type=MESH)
    for near, axis, there in (
        (has_prev, "frame", me - 1), (has_next, "frame", me + 1),
        (has_left, "tensor", mine_z - 1), (has_right, "tensor", mine_z + 1),
    ):
        @pl.when(near)
        def _(axis=axis, there=there):
            pl.semaphore_signal(barrier, inc=1, device_id={axis: there}, device_id_type=MESH)

    for side, near in sides:
        @pl.when(jnp.logical_not(near))
        def _(side=side):
            kv_edge[side] = jnp.zeros(kv_edge.shape[1:], kv_edge.dtype)
            edge_in[:, side] = jnp.zeros(edge_in.shape[:1] + edge_in.shape[2:], edge_in.dtype)

    arrivals = levels
    for near in (has_prev, has_next, has_left, has_right):
        arrivals = arrivals + near.astype(jnp.int32)
    pl.semaphore_wait(barrier, arrivals)

    def z_copy(way, step, part, shard):
        piece_of = gathered.at[shard, aligned(part * chunk, chunk, chunk)]
        return pltpu.make_async_remote_copy(
            src_ref=piece_of,
            dst_ref=piece_of,
            send_sem=z_send.at[way, step, part],
            recv_sem=z_recv.at[way, step, part],
            device_id={"tensor": mine_z + 1 - 2 * way},
            device_id_type=MESH,
        )

    def kv_copy(side, head, source, place):
        return pltpu.make_async_remote_copy(
            src_ref=kv.at[head, :, source],
            dst_ref=kv_edge.at[1 - side, head, :, place],
            send_sem=kv_send.at[side, head],
            recv_sem=kv_recv.at[1 - side, head],
            device_id={"frame": me - 1 + 2 * side},
            device_id_type=MESH,
        )

    own.wait()
    for part in range(rows // chunk):
        for way, near in ways:
            @pl.when(near)
            def _(way=way, part=part):
                z_copy(way, 0, part, mine_z).start()
    for i in (1, 2, 0):
        loads[i].wait()

    def project(shard, part):
        first = shard * rows + part * chunk
        place = aligned(first, chunk, chunk)
        hidden = gathered[shard, aligned(part * chunk, chunk, chunk)]
        raw = dot32(hidden, pool[depth : 2 * depth])
        key_raw[place] = raw
        for head in range(heads):
            one = raw[:, head * HEAD_DIM : (head + 1) * HEAD_DIM]
            kv[head, 0, place] = (one * inverse_rms_of(one) * gain_ref[1:2]).astype(kv.dtype)
        value = dot32(hidden, pool[2 * depth :][:depth]).astype(kv.dtype)
        for head in range(heads):
            kv[head, 1, place] = value[:, head * HEAD_DIM : (head + 1) * HEAD_DIM]
        for side, near in sides:
            @pl.when(near & (first // half == side))
            def _(side=side):
                for head in range(heads):
                    kv_copy(side, head, place, aligned(first - side * half, chunk, chunk)).start()
        query_raw[place] = dot32(hidden, pool[0:depth])
        turned[:, place] = hidden.T

    def one_arrival(index, carry):
        step, part = index // (rows // chunk), index % (rows // chunk)

        @pl.when(step > 0)
        def _():
            for way, near in ways:
                shard = mine_z - step if way == 0 else mine_z + step
                there = shard >= 0 if way == 0 else shard < shards

                @pl.when(there)
                def _(way=way, shard=shard):
                    z_copy(way, step - 1, part, shard).wait_recv()

                @pl.when(there & near)
                def _(way=way, shard=shard):
                    z_copy(way, step, part, shard).start()

        def one_way(way, inner):
            shard = mine_z - step + 2 * step * way

            @pl.when((shard >= 0) & (shard < shards) & (step >= way))
            def _():
                project(shard, part)

            return inner

        return lax.fori_loop(0, 2, one_way, carry)

    lax.fori_loop(0, shards * (rows // chunk), one_arrival, 0)
    for bit in orders[0]:
        pl.semaphore_signal(ready, inc=1, device_id={"frame": flipped(me, bit)}, device_id_type=MESH)

    def columns_of(head):
        return aligned(head * HEAD_DIM, HEAD_DIM, HEAD_DIM)

    def edge_copy(side, head):
        return pltpu.make_async_remote_copy(
            src_ref=edge_out.at[head % 2, side],
            dst_ref=edge_in.at[head % edges, 1 - side],
            send_sem=edge_send.at[head % 2, side],
            recv_sem=edge_recv.at[head % edges, 1 - side],
            device_id={"frame": me - 1 + 2 * side},
            device_id_type=MESH,
        )

    def edge_arrival(side, head):
        return pltpu.make_async_remote_copy(
            src_ref=edge_out.at[head % 2, side],
            dst_ref=edge_in.at[head % edges, side],
            send_sem=edge_send.at[head % 2, side],
            recv_sem=edge_recv.at[head % edges, side],
            device_id={"frame": me - 1 + 2 * side},
            device_id_type=MESH,
        )

    def kv_arrival(side, head):
        return pltpu.make_async_remote_copy(
            src_ref=kv.at[head, :, pl.ds(0, half)],
            dst_ref=kv_edge.at[side, head],
            send_sem=kv_send.at[side, head],
            recv_sem=kv_recv.at[side, head],
            device_id={"frame": me - 1 + 2 * side},
            device_id_type=MESH,
        )

    def attend_block(step):
        head, part = step // blocks, step % blocks
        slot = head % 2
        columns = columns_of(head)
        queries = aligned(part * block, block, block)
        first, second = slice(0, half), slice(half, 2 * half)
        chunks = [
            (kv_edge.at[0, head, 0], kv_edge.at[0, head, 1], first, bias_prev),
            (kv.at[head, 0], kv.at[head, 1], first, None),
            (kv.at[head, 0], kv.at[head, 1], second, None),
            (kv_edge.at[1, head, 0], kv_edge.at[1, head, 1], first, bias_next),
        ]

        @pl.when(part == 0)
        def _():
            for side, near in sides:
                @pl.when(near)
                def _(side=side):
                    kv_arrival(side, head).wait_recv()
            for i, (k_ref, v_ref, span, _) in enumerate(chunks):
                kt[:, i * half : (i + 1) * half] = k_ref[span].T
                vt[:, i * half : (i + 1) * half] = v_ref[span].T
            dk_acc[slot] = jnp.zeros(dk_acc.shape[1:], jnp.float32)
            dv_acc[slot] = jnp.zeros(dv_acc.shape[1:], jnp.float32)

        raw = query_raw[queries, columns]
        gain = gain_ref[0:1]
        inverse_rms = inverse_rms_of(raw)
        query = (raw * inverse_rms * gain).astype(jnp.bfloat16)
        grad = grad_ref[queries, columns]
        peak = None
        for i, (k_ref, v_ref, span, bias) in enumerate(chunks):
            place = slice(i * half, (i + 1) * half)
            s = dot_nt(k_ref[span], query)
            if bias is not None:
                s = s + bias
            score[place] = s
            top = jnp.max(s, axis=0, keepdims=True)
            peak = top if peak is None else jnp.maximum(peak, top)
        norm = None
        for i, (k_ref, v_ref, span, _) in enumerate(chunks):
            place = slice(i * half, (i + 1) * half)
            raised = jnp.exp2((score[place] - peak) * scale)
            score[place] = raised
            total = jnp.sum(raised, axis=0, keepdims=True)
            norm = total if norm is None else norm + total
            prob_grad[place] = dot_nt(v_ref[span], grad)
        inverse = 1.0 / norm
        attended = None
        for i in range(4):
            place = slice(i * half, (i + 1) * half)
            w = (score[place] * inverse).astype(jnp.bfloat16)
            weight[place] = w
            term = dot32(vt[:, place], w)
            attended = term if attended is None else attended + term
            dv_acc[slot, place] += dot32(w, grad)
        attended = attended.T.astype(jnp.bfloat16)
        att_ref[queries, columns] = attended
        dots = jnp.sum((grad.astype(jnp.float32) * attended.astype(jnp.float32)).T, axis=0, keepdims=True)
        query_grad = None
        for i in range(4):
            place = slice(i * half, (i + 1) * half)
            ds = (weight[place].astype(jnp.float32) * (prob_grad[place] - dots)).astype(jnp.bfloat16)
            term = dot32(kt[:, place], ds)
            query_grad = term if query_grad is None else query_grad + term
            dk_acc[slot, place] += dot32(ds, query)
        query_grad = query_grad.T * factor
        grads[slot, queries, 0:HEAD_DIM] = norm_back(raw, inverse_rms, gain, query_grad).astype(jnp.bfloat16)

        @pl.when(part == blocks - 1)
        def _():
            for side, near in sides:
                place = slice(side * 3 * half, (side * 3 + 1) * half)

                @pl.when(near)
                def _(side=side, place=place):
                    edge_out[slot, side, 0] = (dk_acc[slot, place] * factor).astype(jnp.bfloat16)
                    edge_out[slot, side, 1] = dv_acc[slot, place].astype(jnp.bfloat16)
                    edge_copy(side, head).start()

    def lanes_of(stream, part):
        first = stream % per * group
        return pl.ds(first + part * HEAD_DIM, (1 + part) * HEAD_DIM)

    def terms_at(head, stream, place, number):
        first = ((head % slots) * (streams // per) + stream // per) * count + place
        return aligned(first * piece, number * piece, piece)

    def landed_at(head, stream, place, number):
        first = ((head % lands) * (streams // per) + stream // per) * (count - 1) + place
        return aligned(landed_base + first * piece, number * piece, piece)

    def first_at(level):
        return count - (count >> level)

    def halving_copy(head, level, stream, part):
        near, far = count >> (level + 1), count >> level
        lanes = lanes_of(stream, part)
        return pltpu.make_async_remote_copy(
            src_ref=pool.at[terms_at(head, stream, near, far - near), lanes],
            dst_ref=pool.at[landed_at(head, stream, first_at(level), near), lanes],
            send_sem=send_sems.at[head % slots, stream, level, part],
            recv_sem=recv_sems.at[head % lands, stream, level, part],
            device_id={"frame": flipped(me, orders[stream][level])},
            device_id_type=MESH,
        )

    def weight_terms(head, part):
        slot = head % 2
        columns = slice(part * HEAD_DIM, (2 * part + 1) * HEAD_DIM)

        def one_pair(pair, carry):
            span = aligned(pair * 4 * piece, 4 * piece, 4 * piece)
            term = dot32(turned[span], grads[slot, :, columns]).astype(pool.dtype)
            for i in range(2):
                frame = 2 * pair + i
                for stream in range(streams):
                    place = 0
                    for bit in orders[stream]:
                        place = 2 * place + (frame // bit + me // bit) % 2
                    first = (2 * i + stream) * piece
                    pool[terms_at(head, stream, place, 1), lanes_of(stream, part)] = term[first : first + piece]
            return carry

        lax.fori_loop(0, count // 2, one_pair, 0)
        for stream in range(streams):
            halving_copy(head, 0, stream, part).start()

    def key_back(head):
        slot = head % 2
        columns = columns_of(head)
        for side, near in sides:
            @pl.when(near)
            def _(side=side):
                edge_arrival(side, head).wait_recv()
        gain = gain_ref[1:2]
        for part in range(2):
            span = slice(part * half, (part + 1) * half)
            inner = slice((part + 1) * half, (part + 2) * half)
            raw = key_raw[span, columns]
            grad = dk_acc[slot, inner] * factor + edge_in[head % edges, part, 0].astype(jnp.float32)
            back = norm_back(raw, inverse_rms_of(raw), gain, grad)
            grads[slot, span, HEAD_DIM : 2 * HEAD_DIM] = back.astype(jnp.bfloat16)
            grad = dv_acc[slot, inner] + edge_in[head % edges, part, 1].astype(jnp.float32)
            grads[slot, span, 2 * HEAD_DIM : 3 * HEAD_DIM] = grad.astype(jnp.bfloat16)
        for side, near in sides:
            @pl.when(near)
            def _(side=side):
                edge_copy(side, head).wait_send()

    def halve(head, level):
        near, far = count >> (level + 1), count >> level
        for part in range(2):
            for stream in range(streams):
                lanes = lanes_of(stream, part)
                halving_copy(head, level - 1, stream, part).wait_recv()
                span = terms_at(head, stream, near, far - near)
                total = pool[span, lanes].astype(jnp.float32)
                for earlier in range(level):
                    total += pool[landed_at(head, stream, first_at(earlier) + near, far - near), lanes].astype(jnp.float32)
                pool[span, lanes] = total.astype(pool.dtype)
                halving_copy(head, level, stream, part).start()

    def out_copy(head, index):
        return pltpu.make_async_copy(
            totals.at[head % 2, :, pl.ds(index * HEAD_DIM, HEAD_DIM)],
            sum_hbm.at[index, :, columns_of(head)],
            out_sems.at[head % 2, index],
        )

    def finish(head):
        @pl.when(head >= 2)
        def _():
            for i in range(3):
                out_copy(head - 2, i).wait()

        for part in range(2):
            for stream in range(streams):
                lanes = lanes_of(stream, part)
                halving_copy(head, levels - 1, stream, part).wait_recv()
                total = pool[terms_at(head, stream, 0, 1), lanes].astype(jnp.float32)
                for earlier in range(levels):
                    total += pool[landed_at(head, stream, first_at(earlier), 1), lanes].astype(jnp.float32)
                totals[head % 2, stream * piece : (stream + 1) * piece, part * HEAD_DIM : (2 * part + 1) * HEAD_DIM] = total
        for i in range(3):
            out_copy(head, i).start()
        for part in range(2):
            for stream in range(streams):
                for level in range(levels):
                    halving_copy(head, level, stream, part).wait_send()

    def one_step(step, carry):
        @pl.when(step < heads * blocks)
        def _():
            attend_block(step)

        def at_stage(since, act):
            head = since // blocks

            @pl.when((since >= 0) & (since % blocks == 0) & (head < heads))
            def _():
                act(head)

        def keys_and_values(head):
            key_back(head)
            weight_terms(head, 1)

        def query_terms(head):
            @pl.when(head == 0)
            def _():
                pl.semaphore_wait(ready, levels)

            weight_terms(head, 0)

        at_stage(step - blocks - lag, keys_and_values)
        for level in range(1, levels):
            at_stage(step - blocks - lag - level, functools.partial(halve, level=level))
        at_stage(step - blocks - lag - levels, finish)
        at_stage(step - blocks + 1, query_terms)
        return carry

    lax.fori_loop(0, heads * blocks + lag + levels + 1, one_step, 0)

    for head in range(max(0, heads - 2), heads):
        for i in range(3):
            out_copy(head, i).wait()
    for side, near in sides:
        @pl.when(near)
        def _(side=side):
            for head in range(heads):
                kv_arrival(side, head).wait_send()
    for step in range(shards - 1):
        for way, near in ways:
            shard = mine_z - step if way == 0 else mine_z + step
            there = shard >= 0 if way == 0 else shard < shards

            @pl.when(there & near)
            def _(way=way, shard=shard, step=step):
                for part in range(rows // chunk):
                    z_copy(way, step, part, shard).wait_send()


def per_device(hidden, qkv_weight, norm_gain, out_grad):
    count, shards = lax.axis_size("frame"), lax.axis_size("tensor")
    rows, depth = hidden.shape
    tokens, local = out_grad.shape
    heads, half = local // HEAD_DIM, tokens // 2
    block = min(512, tokens)
    window = 2 * tokens
    levels = count.bit_length() - 1
    blocks, lag = tokens // block, 1
    slots = -(-(lag + levels + 1) // blocks)
    lands = 2 + -(-lag // blocks) + levels // blocks
    edges = 2 + 2 * -(-lag // blocks)
    piece = depth // count // 2
    per = max(1, min(2, local // (3 * HEAD_DIM)))
    parts = rows // min(128, rows)
    pool_rows = max(3 * depth, (2 // per) * piece * (slots * count + lands * (count - 1)))
    vmem, anywhere = pl.BlockSpec(memory_space=pltpu.VMEM), pl.BlockSpec(memory_space=pl.ANY)
    flops = 12 * tokens * window * local + 12 * tokens * depth * local
    narrow, wide = jnp.bfloat16, jnp.float32
    attended, sums = pl.pallas_call(
        functools.partial(block_kernel, count, shards, slots, lands, lag, per),
        in_specs=[vmem, anywhere, anywhere, vmem],
        out_specs=(vmem, anywhere),
        out_shape=(
            jax.ShapeDtypeStruct((tokens, local), narrow),
            jax.ShapeDtypeStruct((3, depth // count, local), wide),
        ),
        scratch_shapes=[
            pltpu.VMEM((pool_rows, local), narrow),
            pltpu.VMEM((shards, rows, depth), narrow),
            pltpu.VMEM((depth, tokens), narrow),
            pltpu.VMEM((tokens, local), wide),
            pltpu.VMEM((tokens, local), wide),
            pltpu.VMEM((heads, 2, tokens, HEAD_DIM), narrow),
            pltpu.VMEM((2, heads, 2, half, HEAD_DIM), narrow),
            pltpu.VMEM((HEAD_DIM, window), narrow),
            pltpu.VMEM((HEAD_DIM, window), narrow),
            pltpu.VMEM((window, block), wide),
            pltpu.VMEM((window, block), wide),
            pltpu.VMEM((window, block), narrow),
            pltpu.VMEM((2, window, HEAD_DIM), wide),
            pltpu.VMEM((2, window, HEAD_DIM), wide),
            pltpu.VMEM((2, tokens, 3 * HEAD_DIM), narrow),
            pltpu.VMEM((2, 2, 2, half, HEAD_DIM), narrow),
            pltpu.VMEM((edges, 2, 2, half, HEAD_DIM), narrow),
            pltpu.VMEM((2, depth // count, 3 * HEAD_DIM), wide),
            pltpu.SemaphoreType.DMA((3,)),
            pltpu.SemaphoreType.DMA,
            pltpu.SemaphoreType.DMA((2, shards, parts)),
            pltpu.SemaphoreType.DMA((2, shards, parts)),
            pltpu.SemaphoreType.DMA((2, heads)),
            pltpu.SemaphoreType.DMA((2, heads)),
            pltpu.SemaphoreType.DMA((2, 2)),
            pltpu.SemaphoreType.DMA((edges, 2)),
            pltpu.SemaphoreType.DMA((slots, 2, levels, 2)),
            pltpu.SemaphoreType.DMA((lands, 2, levels, 2)),
            pltpu.SemaphoreType.DMA((2, 3)),
            pltpu.SemaphoreType.REGULAR,
        ],
        compiler_params=pltpu.CompilerParams(
            collective_id=0, has_side_effects=True, vmem_limit_bytes=64 * 1024 * 1024
        ),
        cost_estimate=pl.CostEstimate(
            flops=flops, bytes_accessed=16 * tokens * local, transcendentals=tokens * window * heads
        ),
        name="block",
    )(norm_gain, hidden, jnp.transpose(qkv_weight, (1, 0, 2)), out_grad)
    return (attended, jnp.transpose(sums, (1, 0, 2)))


def solution(mesh):
    placed = (P(("frame", "tensor"), None), P(None, None, "tensor"), P(), P("frame", "tensor"))
    return jax.shard_map(
        per_device,
        mesh=mesh,
        in_specs=placed,
        out_specs=(P("frame", "tensor"), P("frame", None, "tensor")),
        check_vma=False,
    )
```

```python
import functools
import math

import jax
import jax.numpy as jnp
from jax import lax
from jax.experimental import pallas as pl
from jax.experimental.pallas import tpu as pltpu
from jax.sharding import PartitionSpec as P

HEAD_DIM = 128
EPSILON = 1e-06
MASKED = -1e30
NT = (((1,), (1,)), ((), ()))


def inverse_rms_of(raw):
    return lax.rsqrt(jnp.mean(raw * raw, axis=-1, keepdims=True) + EPSILON)


def norm_back(raw, inverse_rms, gain, grad):
    weighted = grad * gain
    inner = jnp.mean(raw * weighted, axis=-1, keepdims=True)
    return inverse_rms * weighted - raw * (inverse_rms * inverse_rms * inverse_rms) * inner


def dot32(left, right):
    return jnp.dot(left, right, preferred_element_type=jnp.float32)


def dot_nt(left, right):
    return lax.dot_general(left, right, NT, preferred_element_type=jnp.float32)


MESH = pl.DeviceIdType.MESH


def flipped(index, bit):
    return index + bit - 2 * bit * (index // bit % 2)


def halving_orders(count):
    bits = [1 << i for i in range(count.bit_length() - 1)]
    return [bits, bits[:1] + bits[:0:-1]]


def split_rows(rows):
    return [rows // 2, rows - rows // 2]


def aligned(first, size, unit):
    return pl.ds(pl.multiple_of(first, unit), size)


def block_kernel(
    count, shards, slots, lands, lag, per, gain_ref, hidden_hbm, weight_hbm, grad_ref,
    att_ref, sum_hbm,
    pool, gathered, turned, query_raw, key_raw, kv, kv_edge,
    kt, vt, score, prob_grad, weight, dk_acc, dv_acc, grads, edge_out, edge_in, totals,
    load_sems, own_sem, z_send, z_recv, kv_send, kv_recv, edge_send, edge_recv, send_sems, recv_sems,
    out_sems, ready,
):
    heads, _, tokens, _ = kv.shape
    half = tokens // 2
    rows, depth = gathered.shape[1:]
    block = score.shape[1]
    blocks = tokens // block
    chunk = min(128, rows)
    factor = HEAD_DIM ** (-0.5)
    scale = factor * math.log2(math.e)
    orders = halving_orders(count)
    streams, levels = len(orders), len(orders[0])
    pieces = split_rows(depth // count)
    full = sum(pieces)
    unit = math.gcd(*pieces)
    group = 3 * HEAD_DIM
    edges = edge_in.shape[0]
    landed_base = (2 - per) * slots * count * full
    me, mine_z = lax.axis_index("frame"), lax.axis_index("tensor")
    has_prev, has_next = me > 0, me < count - 1
    has_left, has_right = mine_z > 0, mine_z < shards - 1
    bias_prev = jnp.where(has_prev, 0.0, MASKED).astype(jnp.float32)
    bias_next = jnp.where(has_next, 0.0, MASKED).astype(jnp.float32)
    sides = ((0, has_prev), (1, has_next))
    ways = ((0, has_right), (1, has_left))

    loads = [
        pltpu.make_async_copy(weight_hbm.at[i], pool.at[pl.ds(i * depth, depth)], load_sems.at[i]) for i in range(3)
    ]
    own = pltpu.make_async_copy(hidden_hbm, gathered.at[mine_z], own_sem)
    own.start()
    for i in (1, 2, 0):
        loads[i].start()

    barrier = pltpu.get_barrier_semaphore()
    for bit in orders[0]:
        pl.semaphore_signal(barrier, inc=1, device_id={"frame": flipped(me, bit)}, device_id_type=MESH)
    for near, axis, there in (
        (has_prev, "frame", me - 1), (has_next, "frame", me + 1),
        (has_left, "tensor", mine_z - 1), (has_right, "tensor", mine_z + 1),
    ):
        @pl.when(near)
        def _(axis=axis, there=there):
            pl.semaphore_signal(barrier, inc=1, device_id={axis: there}, device_id_type=MESH)

    for side, near in sides:
        @pl.when(jnp.logical_not(near))
        def _(side=side):
            kv_edge[side] = jnp.zeros(kv_edge.shape[1:], kv_edge.dtype)
            edge_in[:, side] = jnp.zeros(edge_in.shape[:1] + edge_in.shape[2:], edge_in.dtype)

    arrivals = levels
    for near in (has_prev, has_next, has_left, has_right):
        arrivals = arrivals + near.astype(jnp.int32)
    pl.semaphore_wait(barrier, arrivals)

    def z_copy(way, step, part, shard):
        piece_of = gathered.at[shard, aligned(part * chunk, chunk, chunk)]
        return pltpu.make_async_remote_copy(
            src_ref=piece_of,
            dst_ref=piece_of,
            send_sem=z_send.at[way, step, part],
            recv_sem=z_recv.at[way, step, part],
            device_id={"tensor": mine_z + 1 - 2 * way},
            device_id_type=MESH,
        )

    def kv_copy(side, head, source, place):
        return pltpu.make_async_remote_copy(
            src_ref=kv.at[head, :, source],
            dst_ref=kv_edge.at[1 - side, head, :, place],
            send_sem=kv_send.at[side, head],
            recv_sem=kv_recv.at[1 - side, head],
            device_id={"frame": me - 1 + 2 * side},
            device_id_type=MESH,
        )

    own.wait()
    for part in range(rows // chunk):
        for way, near in ways:
            @pl.when(near)
            def _(way=way, part=part):
                z_copy(way, 0, part, mine_z).start()
    for i in (1, 2, 0):
        loads[i].wait()

    def project(shard, part):
        first = shard * rows + part * chunk
        place = aligned(first, chunk, chunk)
        hidden = gathered[shard, aligned(part * chunk, chunk, chunk)]
        raw = dot32(hidden, pool[depth : 2 * depth])
        key_raw[place] = raw
        for head in range(heads):
            one = raw[:, head * HEAD_DIM : (head + 1) * HEAD_DIM]
            kv[head, 0, place] = (one * inverse_rms_of(one) * gain_ref[1:2]).astype(kv.dtype)
        value = dot32(hidden, pool[2 * depth :][:depth]).astype(kv.dtype)
        for head in range(heads):
            kv[head, 1, place] = value[:, head * HEAD_DIM : (head + 1) * HEAD_DIM]
        for side, near in sides:
            @pl.when(near & (first // half == side))
            def _(side=side):
                for head in range(heads):
                    kv_copy(side, head, place, aligned(first - side * half, chunk, chunk)).start()
        query_raw[place] = dot32(hidden, pool[0:depth])
        turned[:, place] = hidden.T

    def one_arrival(index, carry):
        step, part = index // (rows // chunk), index % (rows // chunk)

        @pl.when(step > 0)
        def _():
            for way, near in ways:
                shard = mine_z - step if way == 0 else mine_z + step
                there = shard >= 0 if way == 0 else shard < shards

                @pl.when(there)
                def _(way=way, shard=shard):
                    z_copy(way, step - 1, part, shard).wait_recv()

                @pl.when(there & near)
                def _(way=way, shard=shard):
                    z_copy(way, step, part, shard).start()

        def one_way(way, inner):
            shard = mine_z - step + 2 * step * way

            @pl.when((shard >= 0) & (shard < shards) & (step >= way))
            def _():
                project(shard, part)

            return inner

        return lax.fori_loop(0, 2, one_way, carry)

    lax.fori_loop(0, shards * (rows // chunk), one_arrival, 0)
    for bit in orders[0]:
        pl.semaphore_signal(ready, inc=1, device_id={"frame": flipped(me, bit)}, device_id_type=MESH)

    def columns_of(head):
        return aligned(head * HEAD_DIM, HEAD_DIM, HEAD_DIM)

    def edge_copy(side, head):
        return pltpu.make_async_remote_copy(
            src_ref=edge_out.at[head % 2, side],
            dst_ref=edge_in.at[head % edges, 1 - side],
            send_sem=edge_send.at[head % 2, side],
            recv_sem=edge_recv.at[head % edges, 1 - side],
            device_id={"frame": me - 1 + 2 * side},
            device_id_type=MESH,
        )

    def edge_arrival(side, head):
        return pltpu.make_async_remote_copy(
            src_ref=edge_out.at[head % 2, side],
            dst_ref=edge_in.at[head % edges, side],
            send_sem=edge_send.at[head % 2, side],
            recv_sem=edge_recv.at[head % edges, side],
            device_id={"frame": me - 1 + 2 * side},
            device_id_type=MESH,
        )

    def kv_arrival(side, head):
        return pltpu.make_async_remote_copy(
            src_ref=kv.at[head, :, pl.ds(0, half)],
            dst_ref=kv_edge.at[side, head],
            send_sem=kv_send.at[side, head],
            recv_sem=kv_recv.at[side, head],
            device_id={"frame": me - 1 + 2 * side},
            device_id_type=MESH,
        )

    def attend_block(step):
        head, part = step // blocks, step % blocks
        slot = head % 2
        columns = columns_of(head)
        queries = aligned(part * block, block, block)
        first, second = slice(0, half), slice(half, 2 * half)
        chunks = [
            (kv_edge.at[0, head, 0], kv_edge.at[0, head, 1], first, bias_prev),
            (kv.at[head, 0], kv.at[head, 1], first, None),
            (kv.at[head, 0], kv.at[head, 1], second, None),
            (kv_edge.at[1, head, 0], kv_edge.at[1, head, 1], first, bias_next),
        ]

        @pl.when(part == 0)
        def _():
            for side, near in sides:
                @pl.when(near)
                def _(side=side):
                    kv_arrival(side, head).wait_recv()
            for i, (k_ref, v_ref, span, _) in enumerate(chunks):
                kt[:, i * half : (i + 1) * half] = k_ref[span].T
                vt[:, i * half : (i + 1) * half] = v_ref[span].T
            dk_acc[slot] = jnp.zeros(dk_acc.shape[1:], jnp.float32)
            dv_acc[slot] = jnp.zeros(dv_acc.shape[1:], jnp.float32)

        raw = query_raw[queries, columns]
        gain = gain_ref[0:1]
        inverse_rms = inverse_rms_of(raw)
        query = (raw * inverse_rms * gain).astype(jnp.bfloat16)
        grad = grad_ref[queries, columns]
        peak = None
        for i, (k_ref, v_ref, span, bias) in enumerate(chunks):
            place = slice(i * half, (i + 1) * half)
            s = dot_nt(k_ref[span], query)
            if bias is not None:
                s = s + bias
            score[place] = s
            top = jnp.max(s, axis=0, keepdims=True)
            peak = top if peak is None else jnp.maximum(peak, top)
        norm = None
        for i, (k_ref, v_ref, span, _) in enumerate(chunks):
            place = slice(i * half, (i + 1) * half)
            raised = jnp.exp2((score[place] - peak) * scale)
            score[place] = raised
            total = jnp.sum(raised, axis=0, keepdims=True)
            norm = total if norm is None else norm + total
            prob_grad[place] = dot_nt(v_ref[span], grad)
        inverse = 1.0 / norm
        attended = None
        for i in range(4):
            place = slice(i * half, (i + 1) * half)
            w = (score[place] * inverse).astype(jnp.bfloat16)
            weight[place] = w
            term = dot32(vt[:, place], w)
            attended = term if attended is None else attended + term
            dv_acc[slot, place] += dot32(w, grad)
        attended = attended.T.astype(jnp.bfloat16)
        att_ref[queries, columns] = attended
        dots = jnp.sum((grad.astype(jnp.float32) * attended.astype(jnp.float32)).T, axis=0, keepdims=True)
        query_grad = None
        for i in range(4):
            place = slice(i * half, (i + 1) * half)
            ds = (weight[place].astype(jnp.float32) * (prob_grad[place] - dots)).astype(jnp.bfloat16)
            term = dot32(kt[:, place], ds)
            query_grad = term if query_grad is None else query_grad + term
            dk_acc[slot, place] += dot32(ds, query)
        query_grad = query_grad.T * factor
        grads[slot, queries, 0:HEAD_DIM] = norm_back(raw, inverse_rms, gain, query_grad).astype(jnp.bfloat16)

        @pl.when(part == blocks - 1)
        def _():
            for side, near in sides:
                place = slice(side * 3 * half, (side * 3 + 1) * half)

                @pl.when(near)
                def _(side=side, place=place):
                    edge_out[slot, side, 0] = (dk_acc[slot, place] * factor).astype(jnp.bfloat16)
                    edge_out[slot, side, 1] = dv_acc[slot, place].astype(jnp.bfloat16)
                    edge_copy(side, head).start()

    def lanes_of(part, landed=False):
        first = (per - 1) * group if landed else 0
        return pl.ds(first + part * HEAD_DIM, (1 + part) * HEAD_DIM)

    def terms_at(head, stream, place, number):
        first = (head % slots) * count * full + stream * count * pieces[0] + place * pieces[stream]
        return aligned(first, number * pieces[stream], unit)

    def landed_at(head, stream, place, number):
        first = (head % lands) * (count - 1) * full + stream * (count - 1) * pieces[0] + place * pieces[stream]
        return aligned(landed_base + first, number * pieces[stream], unit)

    def first_at(level):
        return count - (count >> level)

    def halving_copy(head, level, stream, part):
        near, far = count >> (level + 1), count >> level
        return pltpu.make_async_remote_copy(
            src_ref=pool.at[terms_at(head, stream, near, far - near), lanes_of(part)],
            dst_ref=pool.at[landed_at(head, stream, first_at(level), near), lanes_of(part, True)],
            send_sem=send_sems.at[head % slots, stream, level, part],
            recv_sem=recv_sems.at[head % lands, stream, level, part],
            device_id={"frame": flipped(me, orders[stream][level])},
            device_id_type=MESH,
        )

    def weight_terms(head, part):
        slot = head % 2
        columns = slice(part * HEAD_DIM, (2 * part + 1) * HEAD_DIM)

        def one_pair(pair, carry):
            span = aligned(pair * 2 * full, 2 * full, 2 * full)
            term = dot32(turned[span], grads[slot, :, columns]).astype(pool.dtype)
            for i in range(2):
                frame = 2 * pair + i
                for stream in range(streams):
                    place = 0
                    for bit in orders[stream]:
                        place = 2 * place + (frame // bit + me // bit) % 2
                    first = i * full + stream * pieces[0]
                    pool[terms_at(head, stream, place, 1), lanes_of(part)] = term[first : first + pieces[stream]]
            return carry

        lax.fori_loop(0, count // 2, one_pair, 0)
        for stream in range(streams):
            halving_copy(head, 0, stream, part).start()

    def key_back(head):
        slot = head % 2
        columns = columns_of(head)
        for side, near in sides:
            @pl.when(near)
            def _(side=side):
                edge_arrival(side, head).wait_recv()
        gain = gain_ref[1:2]
        for part in range(2):
            span = slice(part * half, (part + 1) * half)
            inner = slice((part + 1) * half, (part + 2) * half)
            raw = key_raw[span, columns]
            grad = dk_acc[slot, inner] * factor + edge_in[head % edges, part, 0].astype(jnp.float32)
            back = norm_back(raw, inverse_rms_of(raw), gain, grad)
            grads[slot, span, HEAD_DIM : 2 * HEAD_DIM] = back.astype(jnp.bfloat16)
            grad = dv_acc[slot, inner] + edge_in[head % edges, part, 1].astype(jnp.float32)
            grads[slot, span, 2 * HEAD_DIM : 3 * HEAD_DIM] = grad.astype(jnp.bfloat16)
        for side, near in sides:
            @pl.when(near)
            def _(side=side):
                edge_copy(side, head).wait_send()

    def halve(head, level, part):
        near, far = count >> (level + 1), count >> level
        for stream in range(streams):
            halving_copy(head, level - 1, stream, part).wait_recv()
            span = terms_at(head, stream, near, far - near)
            total = pool[span, lanes_of(part)].astype(jnp.float32)
            for earlier in range(level):
                landed = landed_at(head, stream, first_at(earlier) + near, far - near)
                total += pool[landed, lanes_of(part, True)].astype(jnp.float32)
            pool[span, lanes_of(part)] = total.astype(pool.dtype)
            halving_copy(head, level, stream, part).start()

    def out_copy(head, index):
        return pltpu.make_async_copy(
            totals.at[head % 2, :, pl.ds(index * HEAD_DIM, HEAD_DIM)],
            sum_hbm.at[index, :, columns_of(head)],
            out_sems.at[head % 2, index],
        )

    def finish(head):
        @pl.when(head >= 2)
        def _():
            for i in range(3):
                out_copy(head - 2, i).wait()

        for part in range(2):
            for stream in range(streams):
                halving_copy(head, levels - 1, stream, part).wait_recv()
                total = pool[terms_at(head, stream, 0, 1), lanes_of(part)].astype(jnp.float32)
                for earlier in range(levels):
                    landed = landed_at(head, stream, first_at(earlier), 1)
                    total += pool[landed, lanes_of(part, True)].astype(jnp.float32)
                first = stream * pieces[0]
                totals[head % 2, first : first + pieces[stream], part * HEAD_DIM : (2 * part + 1) * HEAD_DIM] = total
        for i in range(3):
            out_copy(head, i).start()
        for part in range(2):
            for stream in range(streams):
                for level in range(levels):
                    halving_copy(head, level, stream, part).wait_send()

    def one_step(step, carry):
        @pl.when(step < heads * blocks)
        def _():
            attend_block(step)

        def at_stage(since, act):
            head = since // blocks

            @pl.when((since >= 0) & (since % blocks == 0) & (head < heads))
            def _():
                act(head)

        def keys_and_values(head):
            key_back(head)
            weight_terms(head, 1)

        def query_terms(head):
            @pl.when(head == 0)
            def _():
                pl.semaphore_wait(ready, levels)

            weight_terms(head, 0)

        at_stage(step - blocks - lag, keys_and_values)
        for level in range(1, levels):
            for part in range(2):
                since = step - blocks + 1 - (lag + 1) * part - level
                at_stage(since, functools.partial(halve, level=level, part=part))
        at_stage(step - blocks - lag - levels - 1, finish)
        at_stage(step - blocks + 1, query_terms)
        return carry

    lax.fori_loop(0, heads * blocks + lag + levels + 2, one_step, 0)

    for head in range(max(0, heads - 2), heads):
        for i in range(3):
            out_copy(head, i).wait()
    for side, near in sides:
        @pl.when(near)
        def _(side=side):
            for head in range(heads):
                kv_arrival(side, head).wait_send()
    for step in range(shards - 1):
        for way, near in ways:
            shard = mine_z - step if way == 0 else mine_z + step
            there = shard >= 0 if way == 0 else shard < shards

            @pl.when(there & near)
            def _(way=way, shard=shard, step=step):
                for part in range(rows // chunk):
                    z_copy(way, step, part, shard).wait_send()


def deliver_kernel(near_ref, far_ref, near_out, far_out, near, far, in_sems, out_sems):
    steps = []
    for source, held, target in ((near_ref, near, near_out), (far_ref, far, far_out)):
        rows = source.shape[0] // 4
        for i in range(4):
            place, n = pl.ds(i * rows, rows), len(steps)
            steps.append((
                pltpu.make_async_copy(source.at[place], held.at[place], in_sems.at[n]),
                pltpu.make_async_copy(held.at[place], target.at[place], out_sems.at[n]),
            ))
    for first, _ in steps:
        first.start()
    for first, second in steps:
        first.wait()
        second.start()
    for _, second in steps:
        second.wait()


def deliver(near, far):
    anywhere = pl.BlockSpec(memory_space=pl.ANY)
    return pl.pallas_call(
        deliver_kernel,
        in_specs=[anywhere] * 2,
        out_specs=(anywhere,) * 2,
        out_shape=tuple(jax.ShapeDtypeStruct(a.shape, a.dtype) for a in (near, far)),
        scratch_shapes=[pltpu.VMEM(a.shape, a.dtype) for a in (near, far)] + [pltpu.SemaphoreType.DMA((8,))] * 2,
        name="deliver",
    )(near, far)


def per_device(hidden, qkv_weight, norm_gain, out_grad):
    count, shards = lax.axis_size("frame"), lax.axis_size("tensor")
    rows, depth = hidden.shape
    tokens, local = out_grad.shape
    heads, half = local // HEAD_DIM, tokens // 2
    block = min(512, tokens)
    window = 2 * tokens
    levels = count.bit_length() - 1
    blocks, lag = tokens // block, 1
    slots = -(-(lag + levels + 2) // blocks)
    lands = slots + 1
    edges = 2 + 2 * -(-lag // blocks)
    per = max(1, min(2, local // (3 * HEAD_DIM)))
    parts = rows // min(128, rows)
    needed = [slots * depth, lands * (count - 1) * (depth // count)]
    pool_rows = max(3 * depth, max(needed) if per == 2 else sum(needed))
    vmem, anywhere = pl.BlockSpec(memory_space=pltpu.VMEM), pl.BlockSpec(memory_space=pl.ANY)
    flops = 12 * tokens * window * local + 12 * tokens * depth * local
    narrow, wide = jnp.bfloat16, jnp.float32
    attended, sums = pl.pallas_call(
        functools.partial(block_kernel, count, shards, slots, lands, lag, per),
        in_specs=[vmem, anywhere, anywhere, vmem],
        out_specs=(vmem, anywhere),
        out_shape=(
            jax.ShapeDtypeStruct((tokens, local), narrow),
            jax.ShapeDtypeStruct((3, depth // count, local), wide),
        ),
        scratch_shapes=[
            pltpu.VMEM((pool_rows, local), narrow),
            pltpu.VMEM((shards, rows, depth), narrow),
            pltpu.VMEM((depth, tokens), narrow),
            pltpu.VMEM((tokens, local), wide),
            pltpu.VMEM((tokens, local), wide),
            pltpu.VMEM((heads, 2, tokens, HEAD_DIM), narrow),
            pltpu.VMEM((2, heads, 2, half, HEAD_DIM), narrow),
            pltpu.VMEM((HEAD_DIM, window), narrow),
            pltpu.VMEM((HEAD_DIM, window), narrow),
            pltpu.VMEM((window, block), wide),
            pltpu.VMEM((window, block), wide),
            pltpu.VMEM((window, block), narrow),
            pltpu.VMEM((2, window, HEAD_DIM), wide),
            pltpu.VMEM((2, window, HEAD_DIM), wide),
            pltpu.VMEM((2, tokens, 3 * HEAD_DIM), narrow),
            pltpu.VMEM((2, 2, 2, half, HEAD_DIM), narrow),
            pltpu.VMEM((edges, 2, 2, half, HEAD_DIM), narrow),
            pltpu.VMEM((2, depth // count, 3 * HEAD_DIM), wide),
            pltpu.SemaphoreType.DMA((3,)),
            pltpu.SemaphoreType.DMA,
            pltpu.SemaphoreType.DMA((2, shards, parts)),
            pltpu.SemaphoreType.DMA((2, shards, parts)),
            pltpu.SemaphoreType.DMA((2, heads)),
            pltpu.SemaphoreType.DMA((2, heads)),
            pltpu.SemaphoreType.DMA((2, 2)),
            pltpu.SemaphoreType.DMA((edges, 2)),
            pltpu.SemaphoreType.DMA((slots, 2, levels, 2)),
            pltpu.SemaphoreType.DMA((lands, 2, levels, 2)),
            pltpu.SemaphoreType.DMA((2, 3)),
            pltpu.SemaphoreType.REGULAR,
        ],
        compiler_params=pltpu.CompilerParams(
            collective_id=0, has_side_effects=True, vmem_limit_bytes=64 * 1024 * 1024
        ),
        cost_estimate=pl.CostEstimate(
            flops=flops, bytes_accessed=16 * tokens * local, transcendentals=tokens * window * heads
        ),
        name="block",
    )(norm_gain, hidden, jnp.transpose(qkv_weight, (1, 0, 2)), out_grad)
    depth_rows = sums.shape[1]
    attended, sums = deliver(attended, sums.reshape(-1, local))
    return (attended, jnp.transpose(sums.reshape(3, depth_rows, local), (1, 0, 2)))


def solution(mesh):
    placed = (P(("frame", "tensor"), None), P(None, None, "tensor"), P(), P("frame", "tensor"))
    return jax.shard_map(
        per_device,
        mesh=mesh,
        in_specs=placed,
        out_specs=(P("frame", "tensor"), P("frame", None, "tensor")),
        check_vma=False,
    )
```

```python
import functools
import math

import jax
import jax.numpy as jnp
from jax import lax
from jax.experimental import pallas as pl
from jax.experimental.pallas import tpu as pltpu
from jax.sharding import PartitionSpec as P

HEAD_DIM = 128
EPSILON = 1e-06
MASKED = -1e30
NT = (((1,), (1,)), ((), ()))


def inverse_rms_of(raw):
    return lax.rsqrt(jnp.mean(raw * raw, axis=-1, keepdims=True) + EPSILON)


def norm_back(raw, inverse_rms, gain, grad):
    weighted = grad * gain
    inner = jnp.mean(raw * weighted, axis=-1, keepdims=True)
    return inverse_rms * weighted - raw * (inverse_rms * inverse_rms * inverse_rms) * inner


def dot32(left, right):
    return jnp.dot(left, right, preferred_element_type=jnp.float32)


def dot_nt(left, right):
    return lax.dot_general(left, right, NT, preferred_element_type=jnp.float32)


MESH = pl.DeviceIdType.MESH


def flipped(index, bit):
    return index + bit - 2 * bit * (index // bit % 2)


def halving_orders(count):
    bits = [1 << i for i in range(count.bit_length() - 1)]
    return [bits, bits[:1] + bits[:0:-1]]


def split_rows(rows):
    return [rows // 2, rows - rows // 2]


def aligned(first, size, unit):
    return pl.ds(pl.multiple_of(first, unit), size)


def block_kernel(
    count, shards, slots, lands, lag, per, gain_ref, hidden_hbm, weight_hbm, grad_hbm,
    att_hbm, sum_hbm,
    grad_ref, att_ref, pool, gathered, turned, query_raw, key_raw, kv, kv_edge,
    kt, vt, score, prob_grad, weight, dk_acc, dv_acc, grads, edge_out, edge_in, totals,
    load_sems, own_sem, z_send, z_recv, kv_send, kv_recv, edge_send, edge_recv, send_sems, recv_sems,
    out_sems, grad_sem, att_sems, ready,
):
    heads, _, tokens, _ = kv.shape
    half = tokens // 2
    rows, depth = gathered.shape[1:]
    block = score.shape[1]
    blocks = tokens // block
    chunk = min(128, rows)
    factor = HEAD_DIM ** (-0.5)
    scale = factor * math.log2(math.e)
    orders = halving_orders(count)
    streams, levels = len(orders), len(orders[0])
    pieces = split_rows(depth // count)
    full = sum(pieces)
    unit = math.gcd(*pieces)
    group = 3 * HEAD_DIM
    edges = edge_in.shape[0]
    landed_base = (2 - per) * slots * count * full
    me, mine_z = lax.axis_index("frame"), lax.axis_index("tensor")
    has_prev, has_next = me > 0, me < count - 1
    has_left, has_right = mine_z > 0, mine_z < shards - 1
    bias_prev = jnp.where(has_prev, 0.0, MASKED).astype(jnp.float32)
    bias_next = jnp.where(has_next, 0.0, MASKED).astype(jnp.float32)
    sides = ((0, has_prev), (1, has_next))
    ways = ((0, has_right), (1, has_left))

    loads = [
        pltpu.make_async_copy(weight_hbm.at[i], pool.at[pl.ds(i * depth, depth)], load_sems.at[i]) for i in range(3)
    ]
    own = pltpu.make_async_copy(hidden_hbm, gathered.at[mine_z], own_sem)
    own.start()
    for i in (1, 2, 0):
        loads[i].start()
    grad_load = pltpu.make_async_copy(grad_hbm, grad_ref, grad_sem)
    grad_load.start()

    barrier = pltpu.get_barrier_semaphore()
    for bit in orders[0]:
        pl.semaphore_signal(barrier, inc=1, device_id={"frame": flipped(me, bit)}, device_id_type=MESH)
    for near, axis, there in (
        (has_prev, "frame", me - 1), (has_next, "frame", me + 1),
        (has_left, "tensor", mine_z - 1), (has_right, "tensor", mine_z + 1),
    ):
        @pl.when(near)
        def _(axis=axis, there=there):
            pl.semaphore_signal(barrier, inc=1, device_id={axis: there}, device_id_type=MESH)

    for side, near in sides:
        @pl.when(jnp.logical_not(near))
        def _(side=side):
            kv_edge[side] = jnp.zeros(kv_edge.shape[1:], kv_edge.dtype)
            edge_in[:, side] = jnp.zeros(edge_in.shape[:1] + edge_in.shape[2:], edge_in.dtype)

    arrivals = levels
    for near in (has_prev, has_next, has_left, has_right):
        arrivals = arrivals + near.astype(jnp.int32)
    pl.semaphore_wait(barrier, arrivals)

    def z_copy(way, step, part, shard):
        piece_of = gathered.at[shard, aligned(part * chunk, chunk, chunk)]
        return pltpu.make_async_remote_copy(
            src_ref=piece_of,
            dst_ref=piece_of,
            send_sem=z_send.at[way, step, part],
            recv_sem=z_recv.at[way, step, part],
            device_id={"tensor": mine_z + 1 - 2 * way},
            device_id_type=MESH,
        )

    def kv_copy(side, head, source, place):
        return pltpu.make_async_remote_copy(
            src_ref=kv.at[head, :, source],
            dst_ref=kv_edge.at[1 - side, head, :, place],
            send_sem=kv_send.at[side, head],
            recv_sem=kv_recv.at[1 - side, head],
            device_id={"frame": me - 1 + 2 * side},
            device_id_type=MESH,
        )

    own.wait()
    for part in range(rows // chunk):
        for way, near in ways:
            @pl.when(near)
            def _(way=way, part=part):
                z_copy(way, 0, part, mine_z).start()
    for i in (1, 2, 0):
        loads[i].wait()
    grad_load.wait()

    def project(shard, part):
        first = shard * rows + part * chunk
        place = aligned(first, chunk, chunk)
        hidden = gathered[shard, aligned(part * chunk, chunk, chunk)]
        raw = dot32(hidden, pool[depth : 2 * depth])
        key_raw[place] = raw
        for head in range(heads):
            one = raw[:, head * HEAD_DIM : (head + 1) * HEAD_DIM]
            kv[head, 0, place] = (one * inverse_rms_of(one) * gain_ref[1:2]).astype(kv.dtype)
        value = dot32(hidden, pool[2 * depth :][:depth]).astype(kv.dtype)
        for head in range(heads):
            kv[head, 1, place] = value[:, head * HEAD_DIM : (head + 1) * HEAD_DIM]
        for side, near in sides:
            @pl.when(near & (first // half == side))
            def _(side=side):
                for head in range(heads):
                    kv_copy(side, head, place, aligned(first - side * half, chunk, chunk)).start()
        query_raw[place] = dot32(hidden, pool[0:depth])
        turned[:, place] = hidden.T

    def one_arrival(index, carry):
        step, part = index // (rows // chunk), index % (rows // chunk)

        @pl.when(step > 0)
        def _():
            for way, near in ways:
                shard = mine_z - step if way == 0 else mine_z + step
                there = shard >= 0 if way == 0 else shard < shards

                @pl.when(there)
                def _(way=way, shard=shard):
                    z_copy(way, step - 1, part, shard).wait_recv()

                @pl.when(there & near)
                def _(way=way, shard=shard):
                    z_copy(way, step, part, shard).start()

        def one_way(way, inner):
            shard = mine_z - step + 2 * step * way

            @pl.when((shard >= 0) & (shard < shards) & (step >= way))
            def _():
                project(shard, part)

            return inner

        return lax.fori_loop(0, 2, one_way, carry)

    lax.fori_loop(0, shards * (rows // chunk), one_arrival, 0)
    for bit in orders[0]:
        pl.semaphore_signal(ready, inc=1, device_id={"frame": flipped(me, bit)}, device_id_type=MESH)

    def columns_of(head):
        return aligned(head * HEAD_DIM, HEAD_DIM, HEAD_DIM)

    def edge_copy(side, head):
        return pltpu.make_async_remote_copy(
            src_ref=edge_out.at[head % 2, side],
            dst_ref=edge_in.at[head % edges, 1 - side],
            send_sem=edge_send.at[head % 2, side],
            recv_sem=edge_recv.at[head % edges, 1 - side],
            device_id={"frame": me - 1 + 2 * side},
            device_id_type=MESH,
        )

    def edge_arrival(side, head):
        return pltpu.make_async_remote_copy(
            src_ref=edge_out.at[head % 2, side],
            dst_ref=edge_in.at[head % edges, side],
            send_sem=edge_send.at[head % 2, side],
            recv_sem=edge_recv.at[head % edges, side],
            device_id={"frame": me - 1 + 2 * side},
            device_id_type=MESH,
        )

    def kv_arrival(side, head):
        return pltpu.make_async_remote_copy(
            src_ref=kv.at[head, :, pl.ds(0, half)],
            dst_ref=kv_edge.at[side, head],
            send_sem=kv_send.at[side, head],
            recv_sem=kv_recv.at[side, head],
            device_id={"frame": me - 1 + 2 * side},
            device_id_type=MESH,
        )

    def att_copy(step):
        place = aligned(step % blocks * block, block, block), columns_of(step // blocks)
        return pltpu.make_async_copy(att_ref.at[place], att_hbm.at[place], att_sems.at[step])

    def attend_block(step):
        head, part = step // blocks, step % blocks
        slot = head % 2
        columns = columns_of(head)
        queries = aligned(part * block, block, block)
        first, second = slice(0, half), slice(half, 2 * half)
        chunks = [
            (kv_edge.at[0, head, 0], kv_edge.at[0, head, 1], first, bias_prev),
            (kv.at[head, 0], kv.at[head, 1], first, None),
            (kv.at[head, 0], kv.at[head, 1], second, None),
            (kv_edge.at[1, head, 0], kv_edge.at[1, head, 1], first, bias_next),
        ]

        @pl.when(part == 0)
        def _():
            for side, near in sides:
                @pl.when(near)
                def _(side=side):
                    kv_arrival(side, head).wait_recv()
            for i, (k_ref, v_ref, span, _) in enumerate(chunks):
                kt[:, i * half : (i + 1) * half] = k_ref[span].T
                vt[:, i * half : (i + 1) * half] = v_ref[span].T
            dk_acc[slot] = jnp.zeros(dk_acc.shape[1:], jnp.float32)
            dv_acc[slot] = jnp.zeros(dv_acc.shape[1:], jnp.float32)

        raw = query_raw[queries, columns]
        gain = gain_ref[0:1]
        inverse_rms = inverse_rms_of(raw)
        query = (raw * inverse_rms * gain).astype(jnp.bfloat16)
        grad = grad_ref[queries, columns]
        peak = None
        for i, (k_ref, v_ref, span, bias) in enumerate(chunks):
            place = slice(i * half, (i + 1) * half)
            s = dot_nt(k_ref[span], query)
            if bias is not None:
                s = s + bias
            score[place] = s
            top = jnp.max(s, axis=0, keepdims=True)
            peak = top if peak is None else jnp.maximum(peak, top)
        norm = None
        for i, (k_ref, v_ref, span, _) in enumerate(chunks):
            place = slice(i * half, (i + 1) * half)
            raised = jnp.exp2((score[place] - peak) * scale)
            score[place] = raised
            total = jnp.sum(raised, axis=0, keepdims=True)
            norm = total if norm is None else norm + total
            prob_grad[place] = dot_nt(v_ref[span], grad)
        inverse = 1.0 / norm
        attended = None
        for i in range(4):
            place = slice(i * half, (i + 1) * half)
            w = (score[place] * inverse).astype(jnp.bfloat16)
            weight[place] = w
            term = dot32(vt[:, place], w)
            attended = term if attended is None else attended + term
            dv_acc[slot, place] += dot32(w, grad)
        attended = attended.T.astype(jnp.bfloat16)
        att_ref[queries, columns] = attended
        att_copy(step).start()
        dots = jnp.sum((grad.astype(jnp.float32) * attended.astype(jnp.float32)).T, axis=0, keepdims=True)
        query_grad = None
        for i in range(4):
            place = slice(i * half, (i + 1) * half)
            ds = (weight[place].astype(jnp.float32) * (prob_grad[place] - dots)).astype(jnp.bfloat16)
            term = dot32(kt[:, place], ds)
            query_grad = term if query_grad is None else query_grad + term
            dk_acc[slot, place] += dot32(ds, query)
        query_grad = query_grad.T * factor
        grads[slot, queries, 0:HEAD_DIM] = norm_back(raw, inverse_rms, gain, query_grad).astype(jnp.bfloat16)

        @pl.when(part == blocks - 1)
        def _():
            for side, near in sides:
                place = slice(side * 3 * half, (side * 3 + 1) * half)

                @pl.when(near)
                def _(side=side, place=place):
                    edge_out[slot, side, 0] = (dk_acc[slot, place] * factor).astype(jnp.bfloat16)
                    edge_out[slot, side, 1] = dv_acc[slot, place].astype(jnp.bfloat16)
                    edge_copy(side, head).start()

    def lanes_of(part, landed=False):
        first = (per - 1) * group if landed else 0
        return pl.ds(first + part * HEAD_DIM, (1 + part) * HEAD_DIM)

    def terms_at(head, stream, place, number):
        first = (head % slots) * count * full + stream * count * pieces[0] + place * pieces[stream]
        return aligned(first, number * pieces[stream], unit)

    def landed_at(head, stream, place, number):
        first = (head % lands) * (count - 1) * full + stream * (count - 1) * pieces[0] + place * pieces[stream]
        return aligned(landed_base + first, number * pieces[stream], unit)

    def first_at(level):
        return count - (count >> level)

    def halving_copy(head, level, stream, part):
        near, far = count >> (level + 1), count >> level
        return pltpu.make_async_remote_copy(
            src_ref=pool.at[terms_at(head, stream, near, far - near), lanes_of(part)],
            dst_ref=pool.at[landed_at(head, stream, first_at(level), near), lanes_of(part, True)],
            send_sem=send_sems.at[head % slots, stream, level, part],
            recv_sem=recv_sems.at[head % lands, stream, level, part],
            device_id={"frame": flipped(me, orders[stream][level])},
            device_id_type=MESH,
        )

    def weight_terms(head, part):
        slot = head % 2
        columns = slice(part * HEAD_DIM, (2 * part + 1) * HEAD_DIM)

        def one_pair(pair, carry):
            span = aligned(pair * 2 * full, 2 * full, 2 * full)
            term = dot32(turned[span], grads[slot, :, columns]).astype(pool.dtype)
            for i in range(2):
                frame = 2 * pair + i
                for stream in range(streams):
                    place = 0
                    for bit in orders[stream]:
                        place = 2 * place + (frame // bit + me // bit) % 2
                    first = i * full + stream * pieces[0]
                    pool[terms_at(head, stream, place, 1), lanes_of(part)] = term[first : first + pieces[stream]]
            return carry

        lax.fori_loop(0, count // 2, one_pair, 0)
        for stream in range(streams):
            halving_copy(head, 0, stream, part).start()

    def key_back(head):
        slot = head % 2
        columns = columns_of(head)
        for side, near in sides:
            @pl.when(near)
            def _(side=side):
                edge_arrival(side, head).wait_recv()
        gain = gain_ref[1:2]
        for part in range(2):
            span = slice(part * half, (part + 1) * half)
            inner = slice((part + 1) * half, (part + 2) * half)
            raw = key_raw[span, columns]
            grad = dk_acc[slot, inner] * factor + edge_in[head % edges, part, 0].astype(jnp.float32)
            back = norm_back(raw, inverse_rms_of(raw), gain, grad)
            grads[slot, span, HEAD_DIM : 2 * HEAD_DIM] = back.astype(jnp.bfloat16)
            grad = dv_acc[slot, inner] + edge_in[head % edges, part, 1].astype(jnp.float32)
            grads[slot, span, 2 * HEAD_DIM : 3 * HEAD_DIM] = grad.astype(jnp.bfloat16)
        for side, near in sides:
            @pl.when(near)
            def _(side=side):
                edge_copy(side, head).wait_send()

    def halve(head, level, part):
        near, far = count >> (level + 1), count >> level
        for stream in range(streams):
            halving_copy(head, level - 1, stream, part).wait_recv()
            span = terms_at(head, stream, near, far - near)
            total = pool[span, lanes_of(part)].astype(jnp.float32)
            for earlier in range(level):
                landed = landed_at(head, stream, first_at(earlier) + near, far - near)
                total += pool[landed, lanes_of(part, True)].astype(jnp.float32)
            pool[span, lanes_of(part)] = total.astype(pool.dtype)
            halving_copy(head, level, stream, part).start()

    def out_copy(head, index):
        return pltpu.make_async_copy(
            totals.at[head % 2, :, pl.ds(index * HEAD_DIM, HEAD_DIM)],
            sum_hbm.at[index, :, columns_of(head)],
            out_sems.at[head % 2, index],
        )

    def finish(head):
        @pl.when(head >= 2)
        def _():
            for i in range(3):
                out_copy(head - 2, i).wait()

        for part in range(2):
            for stream in range(streams):
                halving_copy(head, levels - 1, stream, part).wait_recv()
                total = pool[terms_at(head, stream, 0, 1), lanes_of(part)].astype(jnp.float32)
                for earlier in range(levels):
                    landed = landed_at(head, stream, first_at(earlier), 1)
                    total += pool[landed, lanes_of(part, True)].astype(jnp.float32)
                first = stream * pieces[0]
                totals[head % 2, first : first + pieces[stream], part * HEAD_DIM : (2 * part + 1) * HEAD_DIM] = total
        for i in range(3):
            out_copy(head, i).start()
        for part in range(2):
            for stream in range(streams):
                for level in range(levels):
                    halving_copy(head, level, stream, part).wait_send()

    def one_step(step, carry):
        @pl.when(step < heads * blocks)
        def _():
            attend_block(step)

        def at_stage(since, act):
            head = since // blocks

            @pl.when((since >= 0) & (since % blocks == 0) & (head < heads))
            def _():
                act(head)

        def keys_and_values(head):
            key_back(head)
            weight_terms(head, 1)

        def query_terms(head):
            @pl.when(head == 0)
            def _():
                pl.semaphore_wait(ready, levels)

            weight_terms(head, 0)

        at_stage(step - blocks - lag, keys_and_values)
        for level in range(1, levels):
            for part in range(2):
                since = step - blocks + 1 - (lag + 1) * part - level
                at_stage(since, functools.partial(halve, level=level, part=part))
        at_stage(step - blocks - lag - levels - 1, finish)
        at_stage(step - blocks + 1, query_terms)
        return carry

    lax.fori_loop(0, heads * blocks + lag + levels + 2, one_step, 0)

    for step in range(heads * blocks):
        att_copy(step).wait()
    for head in range(max(0, heads - 2), heads):
        for i in range(3):
            out_copy(head, i).wait()
    for side, near in sides:
        @pl.when(near)
        def _(side=side):
            for head in range(heads):
                kv_arrival(side, head).wait_send()
    for step in range(shards - 1):
        for way, near in ways:
            shard = mine_z - step if way == 0 else mine_z + step
            there = shard >= 0 if way == 0 else shard < shards

            @pl.when(there & near)
            def _(way=way, shard=shard, step=step):
                for part in range(rows // chunk):
                    z_copy(way, step, part, shard).wait_send()


def deliver_kernel(near_ref, far_ref, near_out, far_out, near, far, in_sems, out_sems):
    steps = []
    for source, held, target in ((near_ref, near, near_out), (far_ref, far, far_out)):
        rows = source.shape[0] // 4
        for i in range(4):
            place, n = pl.ds(i * rows, rows), len(steps)
            steps.append((
                pltpu.make_async_copy(source.at[place], held.at[place], in_sems.at[n]),
                pltpu.make_async_copy(held.at[place], target.at[place], out_sems.at[n]),
            ))
    for first, _ in steps:
        first.start()
    for first, second in steps:
        first.wait()
        second.start()
    for _, second in steps:
        second.wait()


def deliver(near, far):
    anywhere = pl.BlockSpec(memory_space=pl.ANY)
    return pl.pallas_call(
        deliver_kernel,
        in_specs=[anywhere] * 2,
        out_specs=(anywhere,) * 2,
        out_shape=tuple(jax.ShapeDtypeStruct(a.shape, a.dtype) for a in (near, far)),
        scratch_shapes=[pltpu.VMEM(a.shape, a.dtype) for a in (near, far)] + [pltpu.SemaphoreType.DMA((8,))] * 2,
        name="deliver",
    )(near, far)


def per_device(hidden, qkv_weight, norm_gain, out_grad):
    count, shards = lax.axis_size("frame"), lax.axis_size("tensor")
    rows, depth = hidden.shape
    tokens, local = out_grad.shape
    heads, half = local // HEAD_DIM, tokens // 2
    block = min(512, tokens)
    window = 2 * tokens
    levels = count.bit_length() - 1
    blocks, lag = tokens // block, 1
    slots = -(-(lag + levels + 2) // blocks)
    lands = slots + 1
    edges = 2 + 2 * -(-lag // blocks)
    per = max(1, min(2, local // (3 * HEAD_DIM)))
    parts = rows // min(128, rows)
    needed = [slots * depth, lands * (count - 1) * (depth // count)]
    pool_rows = max(3 * depth, max(needed) if per == 2 else sum(needed))
    vmem, anywhere = pl.BlockSpec(memory_space=pltpu.VMEM), pl.BlockSpec(memory_space=pl.ANY)
    flops = 12 * tokens * window * local + 12 * tokens * depth * local
    narrow, wide = jnp.bfloat16, jnp.float32
    attended, sums = pl.pallas_call(
        functools.partial(block_kernel, count, shards, slots, lands, lag, per),
        in_specs=[vmem, anywhere, anywhere, anywhere],
        out_specs=(anywhere, anywhere),
        out_shape=(
            jax.ShapeDtypeStruct((tokens, local), narrow),
            jax.ShapeDtypeStruct((3, depth // count, local), wide),
        ),
        scratch_shapes=[
            pltpu.VMEM((tokens, local), narrow),
            pltpu.VMEM((tokens, local), narrow),
            pltpu.VMEM((pool_rows, local), narrow),
            pltpu.VMEM((shards, rows, depth), narrow),
            pltpu.VMEM((depth, tokens), narrow),
            pltpu.VMEM((tokens, local), wide),
            pltpu.VMEM((tokens, local), wide),
            pltpu.VMEM((heads, 2, tokens, HEAD_DIM), narrow),
            pltpu.VMEM((2, heads, 2, half, HEAD_DIM), narrow),
            pltpu.VMEM((HEAD_DIM, window), narrow),
            pltpu.VMEM((HEAD_DIM, window), narrow),
            pltpu.VMEM((window, block), wide),
            pltpu.VMEM((window, block), wide),
            pltpu.VMEM((window, block), narrow),
            pltpu.VMEM((2, window, HEAD_DIM), wide),
            pltpu.VMEM((2, window, HEAD_DIM), wide),
            pltpu.VMEM((2, tokens, 3 * HEAD_DIM), narrow),
            pltpu.VMEM((2, 2, 2, half, HEAD_DIM), narrow),
            pltpu.VMEM((edges, 2, 2, half, HEAD_DIM), narrow),
            pltpu.VMEM((2, depth // count, 3 * HEAD_DIM), wide),
            pltpu.SemaphoreType.DMA((3,)),
            pltpu.SemaphoreType.DMA,
            pltpu.SemaphoreType.DMA((2, shards, parts)),
            pltpu.SemaphoreType.DMA((2, shards, parts)),
            pltpu.SemaphoreType.DMA((2, heads)),
            pltpu.SemaphoreType.DMA((2, heads)),
            pltpu.SemaphoreType.DMA((2, 2)),
            pltpu.SemaphoreType.DMA((edges, 2)),
            pltpu.SemaphoreType.DMA((slots, 2, levels, 2)),
            pltpu.SemaphoreType.DMA((lands, 2, levels, 2)),
            pltpu.SemaphoreType.DMA((2, 3)),
            pltpu.SemaphoreType.DMA,
            pltpu.SemaphoreType.DMA((heads * (tokens // block),)),
            pltpu.SemaphoreType.REGULAR,
        ],
        compiler_params=pltpu.CompilerParams(
            collective_id=0, has_side_effects=True, vmem_limit_bytes=64 * 1024 * 1024
        ),
        cost_estimate=pl.CostEstimate(
            flops=flops, bytes_accessed=16 * tokens * local, transcendentals=tokens * window * heads
        ),
        name="block",
    )(norm_gain, hidden, jnp.transpose(qkv_weight, (1, 0, 2)), out_grad)
    depth_rows = sums.shape[1]
    attended, sums = deliver(attended, sums.reshape(-1, local))
    return (attended, jnp.transpose(sums.reshape(3, depth_rows, local), (1, 0, 2)))


def solution(mesh):
    placed = (P(("frame", "tensor"), None), P(None, None, "tensor"), P(), P("frame", "tensor"))
    return jax.shard_map(
        per_device,
        mesh=mesh,
        in_specs=placed,
        out_specs=(P("frame", "tensor"), P("frame", None, "tensor")),
        check_vma=False,
    )
```
